128 devices in a mesh: ctx: 32 (over x, y, core), head: 4 (over z).
Axes of the slice: x: 4, y: 4, z: 4, core: 2. Of those that a mesh axis runs over, the one named last changes fastest.
Arguments:
- queries: bfloat16 [49152, 1024], P(('ctx', 'head')), may hold values from -30 to 30
- keys: bfloat16 [49152, 1024], P(('ctx', 'head')), may hold values from -30 to 30
- values: bfloat16 [49152, 1024], P(('ctx', 'head')), may hold values from -6 to 6
- directions: bfloat16 [49152, 1024], P(('ctx', 'head')), may hold values from -64 to 64
Outputs:
- attended: bfloat16 [49152, 1024], P(('ctx', 'head'))
The draws below stay inside these ranges and needn't reach their ends.
All inputs are finite; a program needn't handle non-finite values.
Results may differ from the reference program's by a relative error of at most 0.013.
The reference program's roundings to bfloat16 on the way count: a program that leaves them out, or rounds other values in their place, can miss the bound.
Values may be sent and summed in bfloat16 or wider, within the bound.
No kernel may reach another device: no remote copies, remote signals or barrier semaphores. Data moves between devices by JAX's collectives and lax.ppermute only.
A program may use at most 64 MiB of HBM per device.

```python
import math
import jax
import jax.numpy as jnp
from jax import lax

HEADS = 8
DH = 128
TOK_DEV = 1536
HOPS = 3
SUB = 128
TOKENS = 49152
N_CTX = 32


def draw_queries(key, part):
    array = jnp.clip(jax.random.normal(jax.random.fold_in(key, 11), (TOKENS, HEADS * DH), jnp.float32), -4.0, 4.0)
    return jnp.clip(array, -30.0, 30.0).astype(jnp.bfloat16)


def draw_keys(key, part):
    array = jnp.clip(jax.random.normal(jax.random.fold_in(key, 21), (TOKENS, HEADS * DH), jnp.float32), -4.0, 4.0)
    return jnp.clip(array, -30.0, 30.0).astype(jnp.bfloat16)


def draw_directions(key, part):
    array = jnp.clip(jax.random.normal(jax.random.fold_in(key, 31), (TOKENS, HEADS * DH), jnp.float32), -4.0, 4.0)
    row_scale = jnp.exp(jax.random.uniform(jax.random.fold_in(key, 32), (TOKENS, 1), jnp.float32, 0.0, math.log(10.0)))
    array = array * row_scale
    return jnp.clip(array, -64.0, 64.0).astype(jnp.bfloat16)


def shard_levels(stream_key, extent, pieces, low, high):
    def one(position, blocks):
        heights = jax.random.uniform(jax.random.fold_in(jax.random.fold_in(stream_key, 6), position), (blocks,), jnp.float32, low / len(pieces), high / len(pieces))
        return jnp.repeat(jnp.exp(heights), extent[position] // blocks).reshape((-1,) + (1,) * (len(extent) - position - 1))

    loudness = one(*pieces[0])
    for cut in pieces[1:]:
        loudness = loudness * one(*cut)
    return loudness


def normal_values(key, dims, scale, bound, pieces=(), held_as=jnp.bfloat16):
    values = scale * jax.random.normal(key, dims, jnp.float32)
    if pieces:
        values = values * shard_levels(key, dims, pieces, -0.22, 0.18)
    return jnp.clip(values, -bound, bound).astype(held_as)


def setup_inputs(seed: int = 0) -> dict:
    arg_keys = jax.random.split(jax.random.key(seed), 5)
    return {
        "queries": draw_queries(jax.random.fold_in(arg_keys[4], 71), 0),
        "keys": draw_keys(jax.random.fold_in(arg_keys[4], 71), 0),
        "values": normal_values(arg_keys[2], (TOKENS, HEADS * DH), 1.0, 6.0, ((0, 128),)),
        "directions": draw_directions(jax.random.fold_in(arg_keys[4], 71), 0),
    }


highest = lax.Precision.HIGHEST
negative = -1e+30

def unit_rows(raw):
    values32 = raw.astype(jnp.float32)
    return values32 / jnp.sqrt(lax.optimization_barrier(jnp.sum(values32 * values32, axis=-1, keepdims=True)) + 1e-06)

def invert_upper(matrix):
    order = matrix.shape[-1]
    if order == 1:
        return 1.0 / matrix
    half = order // 2
    both = invert_upper(jnp.stack([matrix[..., :half, :half], matrix[..., half:, half:]], 0))
    first_inv = both[0]
    second_inv = both[1]
    corner = jnp.matmul(jnp.matmul(first_inv, matrix[..., :half, half:], precision=highest), second_inv, precision=highest)
    upper_rows = jnp.concatenate([first_inv, -corner], axis=-1)
    lower_rows = jnp.concatenate([jnp.zeros_like(corner), second_inv], axis=-1)
    return jnp.concatenate([upper_rows, lower_rows], axis=-2)

def block_product(normals, inputs):
    length = normals.shape[0]
    width = normals.shape[1]
    gram = jnp.dot(normals, normals.T, precision=highest)
    inverse_t = 0.5 * jnp.eye(length, dtype=jnp.float32) + jnp.triu(gram, 1)
    factor = invert_upper(inverse_t)
    upper = jnp.triu(jnp.ones((length, length), jnp.float32))
    results = []
    for vectors in inputs:
        project = jnp.dot(normals, vectors.T, precision=highest) * upper
        weights = jnp.dot(factor, project, precision=highest)
        results.append(vectors - jnp.dot(weights.T, normals, precision=highest))
    solved = jnp.dot(factor, normals, precision=highest)
    whole = jnp.eye(width, dtype=jnp.float32) - jnp.dot(normals.T, solved, precision=highest)
    return (results, whole)

def shard_frames(raw_dirs, queries, keys):
    length, width = queries.shape
    blocks = length // SUB
    normals = unit_rows(raw_dirs).reshape(blocks, SUB, width)
    query_blocks = queries.astype(jnp.float32).reshape(blocks, SUB, width)
    key_blocks = keys.astype(jnp.float32).reshape(blocks, SUB, width)

    def advance(frame, item):
        moved, whole = block_product(item[0], (item[1], item[2]))
        frame_low = frame.astype(jnp.bfloat16)
        outputs = (jnp.dot(moved[0].astype(jnp.bfloat16), frame_low.T, preferred_element_type=jnp.float32), jnp.dot(moved[1].astype(jnp.bfloat16), frame_low.T, preferred_element_type=jnp.float32))
        return (jnp.dot(frame, whole, precision=highest), outputs)
    final, turned = lax.scan(advance, jnp.eye(width, dtype=jnp.float32), (normals, query_blocks, key_blocks))
    return (final, turned[0].reshape(length, width), turned[1].reshape(length, width).astype(jnp.bfloat16))

def block_stats(query, keys, values, causal):
    scale = 1.0 / math.sqrt(query.shape[-1])
    scores = jnp.einsum('qd,kd->qk', query.astype(jnp.float32), keys.astype(jnp.float32)) * scale
    if causal:
        rows_index = jnp.arange(query.shape[0])
        cols_index = jnp.arange(keys.shape[0])
        scores = jnp.where(rows_index[:, None] >= cols_index[None, :], scores, negative)
    best = lax.optimization_barrier(jnp.max(scores, axis=-1))
    weights = jnp.exp(scores - best[:, None])
    total = lax.optimization_barrier(jnp.sum(weights, axis=-1))
    rounded = weights.astype(jnp.bfloat16).astype(jnp.float32)
    output = jnp.einsum('qk,kd->qd', rounded, values.astype(jnp.float32))
    return (best, output, total)

def combine(state, block, valid):
    best, total_o, total_l = state
    block_best, block_o, block_l = block
    top = jnp.maximum(best, block_best)
    old_scale = jnp.exp(best - top)
    new_scale = jnp.exp(block_best - top)
    merged_o = total_o * old_scale[..., None] + block_o * new_scale[..., None]
    merged_l = total_l * old_scale + block_l * new_scale
    return (jnp.where(valid, top, best), jnp.where(valid, merged_o, total_o), jnp.where(valid, merged_l, total_l))

def reference(queries, keys, values, directions):

    def per_head(array):
        return array.reshape(TOKENS, HEADS, DH).transpose(1, 0, 2).reshape(HEADS, N_CTX, TOK_DEV, DH)

    def one_head(item):
        raw_w, raw_q, raw_k, raw_v = item
        frames, turned, key_turned = lax.map(lambda parts: shard_frames(parts[0], parts[1], parts[2]), (raw_w, raw_q, raw_k))
        frames_low = frames.astype(jnp.bfloat16)

        def one_shard(shard):
            start = turned[shard]
            state = block_stats(start.astype(jnp.bfloat16), key_turned[shard], raw_v[shard], True)
            moving = start
            for distance in range(1, HOPS + 1):
                source = jnp.maximum(shard - distance, 0)
                moving = jnp.dot(moving.astype(jnp.bfloat16), frames_low[source].T, preferred_element_type=jnp.float32)
                block = block_stats(moving.astype(jnp.bfloat16), key_turned[source], raw_v[source], False)
                state = combine(state, block, shard - distance >= 0)
            return (state[1] / state[2][:, None]).astype(jnp.bfloat16)
        return lax.map(one_shard, jnp.arange(N_CTX))
    result = lax.map(one_head, (per_head(directions), per_head(queries), per_head(keys), per_head(values)))
    return result.reshape(HEADS, TOKENS, DH).transpose(1, 0, 2).reshape(TOKENS, HEADS * DH)
```

```python
import math
import jax
import jax.numpy as jnp
from jax import lax
from jax.experimental import pallas as pl
from jax.experimental.pallas import tpu as pltpu
from jax.sharding import PartitionSpec as P

DH = 128
SUB = 128
bf16 = jnp.bfloat16
f32 = jnp.float32
VMEM = pl.BlockSpec(memory_space=pltpu.VMEM)


def dot(a, b):
    return jnp.dot(a, b, preferred_element_type=f32)


def dot_t(a, b):
    return lax.dot_general(a, b, (((1,), (1,)), ((), ())), preferred_element_type=f32)


def halves(x):
    high = x.astype(bf16)
    return high, (x - high.astype(f32)).astype(bf16)


def dot3(a, b):
    return dot(
        jnp.concatenate([a[0], a[1], a[0]], axis=1), jnp.concatenate([b[0], b[0], b[1]], axis=0)
    )


def frames_kernel(w_ref, vh_ref, vl_ref, ft_ref, pt_ref, chain_ref, *, group):
    heads = w_ref.shape[1] // DH
    steps = w_ref.shape[0] // (SUB * group)
    rows = lax.broadcasted_iota(jnp.int32, (SUB, SUB), 0)
    cols = lax.broadcasted_iota(jnp.int32, (SUB, SUB), 1)
    diagonal = rows == cols
    unit = jnp.where(diagonal, 1.0, 0.0).astype(f32)
    for h in range(heads):
        chain_ref[h] = unit

    def one(step, carry):
        pairs = [(g, h) for g in range(group) for h in range(heads)]

        def at(g, h):
            start = pl.multiple_of((step * group + g) * SUB, SUB)
            return (pl.ds(start, SUB), pl.ds(h * DH, DH))

        w = [w_ref[at(*p)] for p in pairs]
        wt = [x.T for x in w]
        gram = [dot(x, t) for x, t in zip(w, wt)]
        lower, inverse = [], []
        for x in gram:
            onto = jnp.where(diagonal, x, 0.0)
            down = 2.0 / (jnp.sum(onto, axis=1, keepdims=True) + 1e-6)
            across = 2.0 / (jnp.sum(onto, axis=0, keepdims=True) + 1e-6)
            near = jnp.where((rows == cols + 1) & (rows % 2 == 1), x, 0.0)
            inverse.append(jnp.where(diagonal, down, 0.0) - near * down * across)
            lower.append(halves(x))
        size = 2
        while size < SUB:
            band = (rows // (2 * size) == cols // (2 * size)) & (rows // size > cols // size)
            split = [halves(x) for x in inverse]
            part = [
                (jnp.where(band, x[0], 0).astype(bf16), jnp.where(band, x[1], 0).astype(bf16))
                for x in lower
            ]
            half = [halves(dot3(x, y)) for x, y in zip(split, part)]
            inverse = [x - dot3(y, z) for x, y, z in zip(inverse, half, split)]
            size *= 2
        split = [halves(x) for x in inverse]
        solved = [
            halves(dot(jnp.concatenate(x, axis=1), jnp.concatenate([y, y], axis=0)))
            for x, y in zip(split, w)
        ]
        whole = [
            halves(unit - dot(jnp.concatenate([t, t], axis=1), jnp.concatenate(v, axis=0)))
            for t, v in zip(wt, solved)
        ]
        for i, p in enumerate(pairs):
            vh_ref[at(*p)] = solved[i][0]
            vl_ref[at(*p)] = solved[i][1]
        frames = [halves(chain_ref[h]) for h in range(heads)]
        for i, p in enumerate(pairs):
            h = p[1]
            ft_ref[at(*p)] = frames[h][0]
            moved = dot3(whole[i], frames[h])
            if p[0] == group - 1:
                chain_ref[h] = moved
            frames[h] = halves(moved)
        return carry

    lax.fori_loop(0, steps, one, 0)
    for h in range(heads):
        pt_ref[:, h * DH : (h + 1) * DH] = chain_ref[h].astype(bf16)


def shard_frames(w, group=2):
    rows, width = w.shape
    shape = jax.ShapeDtypeStruct((rows, width), bf16)
    return pl.pallas_call(
        lambda *refs: frames_kernel(*refs, group=group),
        out_shape=(shape, shape, shape, jax.ShapeDtypeStruct((DH, width), bf16)),
        in_specs=[VMEM],
        out_specs=(VMEM,) * 4,
        scratch_shapes=[pltpu.VMEM((width // DH, DH, DH), f32)],
        name="shard_frames",
    )(w)


def turn_kernel(x_ref, w_ref, vh_ref, vl_ref, ft_ref, pt_ref, o_ref, *, group, tail):
    length, width = x_ref.shape
    heads = width // DH
    rows = lax.broadcasted_iota(jnp.int32, (SUB, SUB), 0)
    cols = lax.broadcasted_iota(jnp.int32, (SUB, SUB), 1)
    seen = rows >= cols

    def one(step, carry):
        places = []
        for g in range(group):
            start = pl.multiple_of((step * group + g) * SUB, SUB)
            places += [(pl.ds(start, SUB), pl.ds(h * DH, DH)) for h in range(heads)]
        x = [x_ref[p] for p in places]
        onto = [halves(jnp.where(seen, dot_t(y, w_ref[p]), 0.0)) for y, p in zip(x, places)]
        turned = [
            (y.astype(f32) - dot3(z, (vh_ref[p], vl_ref[p]))).astype(bf16)
            for y, z, p in zip(x, onto, places)
        ]
        for y, p in zip(turned, places):
            o_ref[p] = dot(y, ft_ref[p]).astype(bf16)
        return carry

    lax.fori_loop(0, length // (SUB * group), one, 0)
    if tail:
        o_ref[length:, :] = pt_ref[...]


def turn(x, w, vh, vl, ft, pt, tail, group=4):
    rows, width = x.shape
    return pl.pallas_call(
        lambda *refs: turn_kernel(*refs, group=group, tail=tail),
        out_shape=jax.ShapeDtypeStruct((rows + (DH if tail else 0), width), bf16),
        in_specs=[VMEM] * 6,
        out_specs=VMEM,
        name="turn_keys" if tail else "turn_queries",
    )(x, w, vh, vl, ft, pt)

SCALE = math.log2(math.e) / math.sqrt(DH)
TILE = 256


def tile_stats(z, k, v, keep=None):
    s = dot_t(z, k)
    if keep is not None:
        s = jnp.where(keep, s, -1e30)
    best = jnp.max(s, axis=1, keepdims=True)
    p = jnp.exp2((s - best) * SCALE).astype(bf16)
    return best, dot(p, jnp.concatenate([v, jnp.ones_like(v)], axis=1))


def pack_stats(columns):
    lane = lax.broadcasted_iota(jnp.int32, (columns[0].shape[0], DH), 1)
    out = jnp.zeros(lane.shape, f32)
    for i, c in enumerate(columns):
        out = jnp.where(lane == i, c, out)
    return out


def local_kernel(q_ref, k_ref, v_ref, acc_ref, stat_ref):
    length, width = q_ref.shape
    heads = width // DH
    for i in range(length // TILE):
        size = (i + 1) * TILE
        rows = lax.broadcasted_iota(jnp.int32, (TILE, size), 0) + i * TILE
        keep = rows >= lax.broadcasted_iota(jnp.int32, (TILE, size), 1)
        columns = []
        for h in range(heads):
            lanes = slice(h * DH, (h + 1) * DH)
            best, both = tile_stats(
                q_ref[i * TILE : size, lanes], k_ref[:size, lanes], v_ref[:size, lanes], keep
            )
            acc_ref[i * TILE : size, lanes] = both[:, :DH]
            columns += [best, both[:, DH : DH + 1]]
        stat_ref[i * TILE : size, :] = pack_stats(columns)


def attend_local(zq, kp, v):
    rows, width = zq.shape
    return pl.pallas_call(
        local_kernel,
        out_shape=(
            jax.ShapeDtypeStruct((rows, width), f32),
            jax.ShapeDtypeStruct((rows, DH), f32),
        ),
        in_specs=[VMEM] * 3,
        out_specs=(VMEM,) * 2,
        name="attend_local",
    )(zq, kp, v)


def hop_kernel(ok_ref, z_ref, k_ref, v_ref, acc_ref, stat_ref, *out, last):
    length, width = z_ref.shape
    heads = width // DH
    ok = ok_ref[0] > 0

    def one(i, carry):
        rows = pl.ds(pl.multiple_of(i * TILE, TILE), TILE)
        columns = []
        for h in range(heads):
            lanes = pl.ds(h * DH, DH)
            z = dot(z_ref[rows, lanes], k_ref[length:, h * DH : (h + 1) * DH]).astype(bf16)
            best, both = tile_stats(z, k_ref[:length, h * DH : (h + 1) * DH], v_ref[:, h * DH : (h + 1) * DH])
            stat = stat_ref[rows, :]
            old = stat[:, 2 * h : 2 * h + 1]
            top = jnp.where(ok, jnp.maximum(old, best), old)
            keep = jnp.exp2((old - top) * SCALE)
            gain = jnp.where(ok, jnp.exp2((best - top) * SCALE), 0.0)
            acc = acc_ref[rows, lanes] * keep + both[:, :DH] * gain
            if last:
                total = stat[:, 2 * h + 1 : 2 * h + 2] * keep + both[:, DH:] * gain
                out[0][rows, lanes] = (acc / total).astype(bf16)
            else:
                out[0][rows, lanes] = acc
                out[2][rows, lanes] = z
                total = stat[:, 2 * h + 1 : 2 * h + 2] * keep + both[:, DH : DH + 1] * gain
                columns += [top, total]
        if not last:
            out[1][rows, :] = pack_stats(columns)
        return carry

    lax.fori_loop(0, length // TILE, one, 0)


def attend_hop(ok, z, kp, v, acc, stat, last):
    rows, width = z.shape
    small = jax.ShapeDtypeStruct((rows, width), bf16)
    shapes = (
        (small,)
        if last
        else (
            jax.ShapeDtypeStruct((rows, width), f32),
            jax.ShapeDtypeStruct((rows, DH), f32),
            small,
        )
    )
    return pl.pallas_call(
        lambda *refs: hop_kernel(*refs, last=last),
        out_shape=shapes,
        in_specs=[pl.BlockSpec(memory_space=pltpu.SMEM)] + [VMEM] * 5,
        out_specs=(VMEM,) * len(shapes),
        name="attend_last" if last else "attend_hop",
    )(ok, z, kp, v, acc, stat)


HOPS = 3


def shift(value, axis, by):
    length = lax.axis_size(axis)
    return lax.ppermute(value, axis, [(i, (i + by) % length) for i in range(length)])


def gather_heads(array):
    parts = lax.axis_size("head")
    here = lax.axis_index("head")
    rows, width = array.shape
    piece = width // parts
    out = jnp.zeros((rows * parts, piece), array.dtype)
    for k in range(parts):
        chunk = lax.dynamic_slice(array, (0, (here + k) % parts * piece), (rows, piece))
        if k:
            chunk = shift(chunk, "head", k)
        out = lax.dynamic_update_slice(out, chunk, ((here + parts - k) % parts * rows, 0))
    return out


def scatter_heads(array):
    parts = lax.axis_size("head")
    here = lax.axis_index("head")
    rows, width = array.shape
    piece = rows // parts
    out = jnp.zeros((piece, width * parts), array.dtype)
    for k in range(parts):
        chunk = lax.dynamic_slice(array, ((here + k) % parts * piece, 0), (piece, width))
        if k:
            chunk = shift(chunk, "head", k)
        out = lax.dynamic_update_slice(out, chunk, (0, (here + parts - k) % parts * width))
    return out


def body(queries, keys, values, directions):
    v = gather_heads(values)
    w = gather_heads(directions)
    k = gather_heads(keys)
    q = gather_heads(queries)
    vh, vl, ft, pt = shard_frames(w, 4)
    kp = turn(k, w, vh, vl, ft, pt, True)
    z = turn(q, w, vh, vl, ft, pt, False)
    acc, stat = attend_local(z, kp, v)
    position = lax.axis_index("ctx")
    for distance in range(1, HOPS + 1):
        v = shift(v, "ctx", 1)
        kp = shift(kp, "ctx", 1)
        ok = (position >= distance).astype(jnp.int32).reshape(1)
        out = attend_hop(ok, z, kp, v, acc, stat, distance == HOPS)
        if distance < HOPS:
            acc, stat, z = out
    return scatter_heads(out[0])


def solution(mesh):
    spec = P(("ctx", "head"), None)
    return jax.shard_map(
        body, mesh=mesh, in_specs=(spec,) * 4, out_specs=spec, check_vma=False
    )
```

```python
import math
import jax
import jax.numpy as jnp
from jax import lax
from jax.experimental import pallas as pl
from jax.experimental.pallas import tpu as pltpu
from jax.sharding import PartitionSpec as P

DH = 128
SUB = 128
bf16 = jnp.bfloat16
f32 = jnp.float32
VMEM = pl.BlockSpec(memory_space=pltpu.VMEM)
SMEM = pl.BlockSpec(memory_space=pltpu.SMEM)
GRANT = 24 << 20
COST = 10**8


near = pltpu.VMEM


def keep_near(x):
    return pltpu.with_memory_space_constraint(x, pltpu.VMEM)


def dot(a, b):
    return jnp.dot(a, b, preferred_element_type=f32)


def dot_t(a, b):
    return lax.dot_general(a, b, (((1,), (1,)), ((), ())), preferred_element_type=f32)


def halves(x):
    high = x.astype(bf16)
    return high, (x - high.astype(f32)).astype(bf16)


def thirds(x):
    high = x.astype(bf16)
    rest = x - high.astype(f32)
    middle = rest.astype(bf16)
    return high, middle, (rest - middle.astype(f32)).astype(bf16)


def dot6(a, b):
    return dot(
        jnp.concatenate([a[0], a[1], a[2], a[0], a[1], a[0]], axis=1),
        jnp.concatenate([b[0], b[0], b[0], b[1], b[1], b[2]], axis=0),
    )


def dot3(a, b):
    return dot(
        jnp.concatenate([a[0], a[1], a[0]], axis=1), jnp.concatenate([b[0], b[0], b[1]], axis=0)
    )


def put_chunks(here_ref, chunks, out_ref):
    here = here_ref[0]
    parts = len(chunks)
    rows = chunks[0].shape[0]
    for k, chunk in enumerate(chunks):
        start = pl.multiple_of((here + parts - k) % parts * rows, rows)
        out_ref[pl.ds(start, rows), :] = chunk[...]


def assemble(here, chunks):
    rows, width = chunks[0].shape
    return pl.pallas_call(
        lambda here_ref, *refs: put_chunks(here_ref, refs[:-1], refs[-1]),
        out_shape=near((rows * len(chunks), width), bf16),
        in_specs=[SMEM] + [VMEM] * len(chunks),
        out_specs=VMEM,
        cost_estimate=pl.CostEstimate(flops=COST, bytes_accessed=COST, transcendentals=COST),
        compiler_params=pltpu.CompilerParams(vmem_limit_bytes=GRANT),
        name="assemble",
    )(here, *map(keep_near, chunks))


def pick_kernel(first_ref, one_ref, two_ref, out_ref):
    @pl.when(first_ref[0] > 0)
    def _():
        out_ref[...] = one_ref[...]

    @pl.when(first_ref[0] == 0)
    def _():
        out_ref[...] = two_ref[...]


def pick(first, one, two):
    return pl.pallas_call(
        pick_kernel,
        out_shape=near(one.shape, one.dtype),
        in_specs=[SMEM] + [VMEM] * 2,
        out_specs=VMEM,
        cost_estimate=pl.CostEstimate(flops=COST, bytes_accessed=COST, transcendentals=COST),
        compiler_params=pltpu.CompilerParams(vmem_limit_bytes=GRANT),
        name="pick",
    )(first, keep_near(one), keep_near(two))


def frames_kernel(*refs, group, first):
    if first:
        here_ref, chunks = refs[0], refs[1:-4]
        v_ref, ft_ref, w_ref, chain_ref = refs[-4:]
        put_chunks(here_ref, chunks, w_ref)
        base = 0
    else:
        w_ref, old_ref, v_ref, ft_ref, pt_ref, chain_ref = refs
        base = w_ref.shape[0] - v_ref.shape[0]
    heads = w_ref.shape[1] // DH
    steps = v_ref.shape[0] // (SUB * group)
    rows = lax.broadcasted_iota(jnp.int32, (SUB, SUB), 0)
    cols = lax.broadcasted_iota(jnp.int32, (SUB, SUB), 1)
    diagonal = rows == cols
    unit = jnp.where(diagonal, 1.0, 0.0).astype(f32)
    for h in range(heads):
        chain_ref[h] = unit if first else old_ref[h]

    def one(step, carry):
        pairs = [(g, h) for g in range(group) for h in range(heads)]

        def at(g, h):
            start = pl.multiple_of((step * group + g) * SUB, SUB)
            return (pl.ds(start, SUB), pl.ds(h * DH, DH))

        def source(g, h):
            start = pl.multiple_of((step * group + g) * SUB + base, SUB)
            return (pl.ds(start, SUB), pl.ds(h * DH, DH))

        w = [w_ref[source(*p)] for p in pairs]
        wt = [x.T for x in w]
        gram = [dot(x, t) for x, t in zip(w, wt)]
        lower, inverse, matrix = [], [], []
        for x in gram:
            onto = jnp.where(diagonal, x, 0.0)
            down = 2.0 / (jnp.sum(onto, axis=1, keepdims=True) + 1e-6)
            across = 2.0 / (jnp.sum(onto, axis=0, keepdims=True) + 1e-6)
            near = jnp.where((rows == cols + 1) & (rows % 2 == 1), x, 0.0)
            inverse.append(jnp.where(diagonal, down, 0.0) - near * down * across)
            lower.append(halves(x))
            matrix.append(jnp.where(rows > cols, x, jnp.where(diagonal, 0.5 * (x + 1e-6), 0.0)))
        size = 2
        while size < SUB:
            band = (rows // (2 * size) == cols // (2 * size)) & (rows // size > cols // size)
            split = [halves(x) for x in inverse]
            part = [
                (jnp.where(band, x[0], 0).astype(bf16), jnp.where(band, x[1], 0).astype(bf16))
                for x in lower
            ]
            half = [halves(dot3(x, y)) for x, y in zip(split, part)]
            inverse = [x - dot3(y, z) for x, y, z in zip(inverse, half, split)]
            size *= 2
        split = [halves(x) for x in inverse]
        guess = [
            dot(jnp.concatenate(x, axis=1), jnp.concatenate([y, y], axis=0))
            for x, y in zip(split, w)
        ]
        short = [
            (y.astype(f32) - dot6(thirds(m), thirds(x))).astype(bf16)
            for m, x, y in zip(matrix, guess, w)
        ]
        solved = [x + dot(y[0], z) for x, y, z in zip(guess, split, short)]
        whole = [
            thirds(
                unit
                - dot(jnp.concatenate([t, t, t], axis=1), jnp.concatenate(thirds(v), axis=0))
            )
            for t, v in zip(wt, solved)
        ]
        for i, p in enumerate(pairs):
            v_ref[at(*p)] = solved[i]
        frames = [thirds(chain_ref[h]) for h in range(heads)]
        for i, p in enumerate(pairs):
            h = p[1]
            ft_ref[at(*p)] = frames[h][0]
            moved = dot6(whole[i], frames[h])
            if p[0] == group - 1:
                chain_ref[h] = moved
            frames[h] = thirds(moved)
        return carry

    lax.fori_loop(0, steps, one, 0)
    if not first:
        for h in range(heads):
            pt_ref[:, h * DH : (h + 1) * DH] = chain_ref[h].astype(bf16)


def first_frames(here, chunks, group=3):
    rows, width = chunks[0].shape
    rows *= len(chunks)
    half = rows // 2
    return pl.pallas_call(
        lambda *refs: frames_kernel(*refs, group=group, first=True),
        out_shape=(
            near((half, width), f32),
            near((half, width), bf16),
            near((rows, width), bf16),
            near((width // DH, DH, DH), f32),
        ),
        in_specs=[SMEM] + [VMEM] * len(chunks),
        out_specs=(VMEM,) * 4,
        cost_estimate=pl.CostEstimate(flops=COST, bytes_accessed=COST, transcendentals=COST),
        compiler_params=pltpu.CompilerParams(vmem_limit_bytes=GRANT),
        name="first_frames",
    )(here, *map(keep_near, chunks))


def second_frames(w, chain, group=3):
    rows, width = w.shape
    half = rows // 2
    return pl.pallas_call(
        lambda *refs: frames_kernel(*refs, group=group, first=False),
        out_shape=(
            near((half, width), f32),
            near((half, width), bf16),
            near((DH, width), bf16),
        ),
        in_specs=[VMEM] * 2,
        out_specs=(VMEM,) * 3,
        scratch_shapes=[pltpu.VMEM((width // DH, DH, DH), f32)],
        cost_estimate=pl.CostEstimate(flops=COST, bytes_accessed=COST, transcendentals=COST),
        compiler_params=pltpu.CompilerParams(vmem_limit_bytes=GRANT),
        name="second_frames",
    )(keep_near(w), keep_near(chain))


def turn_kernel(here_ref, *refs, group, tail):
    chunks, (w_ref, v0_ref, ft0_ref, v1_ref, ft1_ref, pt_ref, o_ref, x_ref) = refs[:-8], refs[-8:]
    put_chunks(here_ref, chunks, x_ref)
    length, width = x_ref.shape
    heads = width // DH
    half = length // 2
    rows = lax.broadcasted_iota(jnp.int32, (SUB, SUB), 0)
    cols = lax.broadcasted_iota(jnp.int32, (SUB, SUB), 1)
    seen = rows >= cols

    def one(step, base, v_ref, ft_ref):
        places, inner = [], []
        for g in range(group):
            start = pl.multiple_of((step * group + g) * SUB, SUB)
            for h in range(heads):
                inner.append((pl.ds(start, SUB), pl.ds(h * DH, DH)))
                places.append((pl.ds(start + base, SUB), pl.ds(h * DH, DH)))
        x = [x_ref[p] for p in places]
        onto = [thirds(jnp.where(seen, dot_t(y, w_ref[p]), 0.0)) for y, p in zip(x, places)]
        turned = [
            (y.astype(f32) - dot6(z, thirds(v_ref[p]))).astype(bf16)
            for y, z, p in zip(x, onto, inner)
        ]
        for y, p, i in zip(turned, places, inner):
            o_ref[p] = dot(y, ft_ref[i]).astype(bf16)

    for base, v_ref, ft_ref in ((0, v0_ref, ft0_ref), (half, v1_ref, ft1_ref)):

        def loop(step, carry):
            one(step, base, v_ref, ft_ref)
            return carry

        lax.fori_loop(0, half // (SUB * group), loop, 0)
    if tail:
        o_ref[length:, :] = pt_ref[...]


def turn(here, chunks, w, parts, pt, tail, group=2):
    rows, width = w.shape
    return pl.pallas_call(
        lambda *refs: turn_kernel(*refs, group=group, tail=tail),
        out_shape=near((rows + (DH if tail else 0), width), bf16),
        in_specs=[SMEM] + [VMEM] * (6 + len(chunks)),
        out_specs=VMEM,
        scratch_shapes=[pltpu.VMEM((rows, width), bf16)],
        cost_estimate=pl.CostEstimate(flops=COST, bytes_accessed=COST, transcendentals=COST),
        compiler_params=pltpu.CompilerParams(vmem_limit_bytes=GRANT),
        name="turn_keys" if tail else "turn_queries",
    )(here, *map(keep_near, (*chunks, w, *parts, pt)))


SCALE = math.log2(math.e) / math.sqrt(DH)
TILE = 256
SPAN = 256

BLANK = -1e30


def lanes_of(h):
    return slice(h * DH, (h + 1) * DH)


def pack_stats(columns):
    lane = lax.broadcasted_iota(jnp.int32, (columns[0].shape[0], DH), 1)
    out = jnp.zeros(lane.shape, f32)
    for i, c in enumerate(columns):
        out = jnp.where(lane == i, c, out)
    return out


def score(z, k, s_ref, m_ref, start=None):
    s = dot_t(z, k)
    rows, size = s.shape
    if start is not None:
        low = s[:, : size - rows]
        edge = s[:, size - rows :]
        seen = lax.broadcasted_iota(jnp.int32, edge.shape, 0) >= lax.broadcasted_iota(
            jnp.int32, edge.shape, 1
        )
        edge = jnp.where(seen, edge, BLANK)
        s = jnp.concatenate([low, edge], axis=1) if size > rows else edge
    s_ref[:, :size] = s
    m_ref[...] = jnp.broadcast_to(jnp.max(s, axis=1, keepdims=True), m_ref.shape)


def weigh(v, s_ref, m_ref):
    size = v.shape[0]
    best = m_ref[:, :1]
    p = jnp.exp2((s_ref[:, :size] - best) * SCALE).astype(bf16)
    return best, dot(p, jnp.concatenate([v, jnp.ones_like(v)], axis=1))


def scratch(heads, length, tile):
    return [pltpu.VMEM((tile, length), f32) for _ in range(heads)] + [
        pltpu.VMEM((tile, DH), f32) for _ in range(heads)
    ]


def local_kernel(q_ref, k_ref, v_ref, acc_ref, stat_ref, *work):
    length, width = q_ref.shape
    heads = width // DH
    tiles = length // TILE

    def first(i, h):
        size = (i + 1) * TILE
        score(
            q_ref[i * TILE : size, lanes_of(h)],
            k_ref[:size, lanes_of(h)],
            work[h],
            work[heads + h],
            i * TILE,
        )

    order = [(i, h) for i in range(tiles) for h in range(heads)]
    first(*order[0])
    columns = []
    for n, (i, h) in enumerate(order):
        if n + 1 < len(order):
            first(*order[n + 1])
        size = (i + 1) * TILE
        best, both = weigh(v_ref[:size, lanes_of(h)], work[h], work[heads + h])
        acc_ref[i * TILE : size, lanes_of(h)] = both[:, :DH]
        columns += [best, both[:, DH : DH + 1]]
        if h == heads - 1:
            stat_ref[i * TILE : size, :] = pack_stats(columns)
            columns = []


def attend_local(zq, kp, v):
    rows, width = zq.shape
    return pl.pallas_call(
        local_kernel,
        out_shape=(
            near((rows, width), f32),
            near((rows, DH), f32),
        ),
        in_specs=[VMEM] * 3,
        out_specs=(VMEM,) * 2,
        scratch_shapes=scratch(width // DH, rows, TILE),
        cost_estimate=pl.CostEstimate(flops=COST, bytes_accessed=COST, transcendentals=COST),
        compiler_params=pltpu.CompilerParams(vmem_limit_bytes=GRANT),
        name="attend_local",
    )(keep_near(zq), keep_near(kp), keep_near(v))


def merge(ok, best, both, stat, acc, h, wide):
    old = stat[:, 2 * h : 2 * h + 1]
    top = jnp.where(ok, jnp.maximum(old, best), old)
    keep = jnp.exp2((old - top) * SCALE)
    gain = jnp.where(ok, jnp.exp2((best - top) * SCALE), 0.0)
    sums = both[:, DH:] if wide else both[:, DH : DH + 1]
    total = stat[:, 2 * h + 1 : 2 * h + 2] * keep + sums * gain
    return top, acc * keep + both[:, :DH] * gain, total


def hop_kernel(ok_ref, z_ref, k_ref, v_ref, acc_ref, stat_ref, out_ref, total_ref, turned_ref, *work):
    length, width = z_ref.shape
    heads = width // DH
    tiles = length // SPAN
    ok = ok_ref[0] > 0
    for h in range(heads):
        turned_ref[:, lanes_of(h)] = dot(z_ref[:, lanes_of(h)], k_ref[length:, lanes_of(h)]).astype(
            bf16
        )

    def rows_of(i):
        return pl.ds(pl.multiple_of(i * SPAN, SPAN), SPAN)

    def first(i, h):
        score(turned_ref[rows_of(i), lanes_of(h)], k_ref[:length, lanes_of(h)], work[h], work[heads + h])

    def one(i, more):
        columns = []
        for h in range(heads):
            if h + 1 < heads:
                first(i, h + 1)
            elif more:
                first(i + 1, 0)
            best, both = weigh(v_ref[:, lanes_of(h)], work[h], work[heads + h])
            top, acc, total = merge(
                ok, best, both, stat_ref[rows_of(i), :], acc_ref[rows_of(i), lanes_of(h)], h, False
            )
            out_ref[rows_of(i), lanes_of(h)] = acc
            columns += [top, total]
        total_ref[rows_of(i), :] = pack_stats(columns)

    first(0, 0)

    def step(i, carry):
        one(i, True)
        return carry

    lax.fori_loop(0, tiles - 1, step, 0)
    one(tiles - 1, False)


def attend_hop(ok, z, kp, v, acc, stat):
    rows, width = z.shape
    return pl.pallas_call(
        hop_kernel,
        out_shape=(near((rows, width), f32), near((rows, DH), f32), near((rows, width), bf16)),
        in_specs=[SMEM] + [VMEM] * 5,
        out_specs=(VMEM,) * 3,
        scratch_shapes=scratch(width // DH, rows, SPAN),
        cost_estimate=pl.CostEstimate(flops=COST, bytes_accessed=COST, transcendentals=COST),
        compiler_params=pltpu.CompilerParams(vmem_limit_bytes=GRANT),
        name="attend_hop",
    )(ok, *map(keep_near, (z, kp, v, acc, stat)))


def last_kernel(ok_ref, here_ref, z_ref, *refs, targets, parts):
    pairs, refs = (refs[:2], refs[2:4]), refs[4:]
    acc_ref, stat_ref, out, work = refs[0], refs[1], refs[2 : 2 + len(targets)], refs[2 + len(targets) :]
    done_ref, turned_ref, work = work[0], work[1], work[2:]
    length, width = z_ref.shape
    heads = width // DH
    piece = length // parts
    order = [(d, h) for d in range(len(pairs)) for h in range(heads)]

    def rows_of(i):
        return pl.ds(pl.multiple_of((here_ref[0] + targets[0] + i) % parts * piece, piece), piece)

    def first(i, d, h):
        k_ref = pairs[d][0]
        old = turned_ref[:, lanes_of(h)] if d else z_ref[rows_of(i), lanes_of(h)]
        z = dot(old, k_ref[length:, lanes_of(h)]).astype(bf16)
        turned_ref[:, lanes_of(h)] = z
        score(z, k_ref[:length, lanes_of(h)], work[h], work[heads + h])

    def one(i, carry):
        state = [None] * heads
        for n, (d, h) in enumerate(order):
            if n + 1 < len(order):
                first(i, *order[n + 1])
            elif len(targets) > 1:
                first(jnp.minimum(i + 1, len(targets) - 1), *order[0])
            best, both = weigh(pairs[d][1][:, lanes_of(h)], work[h], work[heads + h])
            if d == 0:
                stat = stat_ref[rows_of(i), :]
                old = stat[:, 2 * h : 2 * h + 1]
                total = stat[:, 2 * h + 1 : 2 * h + 2]
                acc = acc_ref[rows_of(i), lanes_of(h)]
            else:
                old, acc, total = state[h]
            ok = ok_ref[d] > 0
            top = jnp.where(ok, jnp.maximum(old, best), old)
            keep = jnp.exp2((old - top) * SCALE)
            gain = jnp.where(ok, jnp.exp2((best - top) * SCALE), 0.0)
            acc = acc * keep + both[:, :DH] * gain
            total = total * keep + both[:, DH:] * gain
            state[h] = (top, acc, total)
            if d == len(pairs) - 1:
                done_ref[i, :, lanes_of(h)] = (acc / total).astype(bf16)
        return carry

    first(0, *order[0])
    lax.fori_loop(0, len(targets), one, 0)
    for i in range(len(targets)):
        out[i][...] = done_ref[i]


def attend_last(ok, here, z, near_pair, far_pair, acc, stat, targets, parts):
    rows, width = z.shape
    piece = rows // parts
    return pl.pallas_call(
        lambda *refs: last_kernel(*refs, targets=targets, parts=parts),
        out_shape=tuple(near((piece, width), bf16) for _ in targets),
        in_specs=[SMEM] * 2 + [VMEM] * 7,
        out_specs=(VMEM,) * len(targets),
        scratch_shapes=[
            pltpu.VMEM((len(targets), piece, width), bf16),
            pltpu.VMEM((piece, width), bf16),
        ]
        + scratch(width // DH, rows, piece),
        cost_estimate=pl.CostEstimate(flops=COST, bytes_accessed=COST, transcendentals=COST),
        compiler_params=pltpu.CompilerParams(vmem_limit_bytes=GRANT),
    )(ok, here, *map(keep_near, (z, *near_pair, *far_pair, acc, stat)))


HOPS = 3
CORES = 2
LINE = 4


def shift(value, axis, by):
    length = lax.axis_size(axis)
    return lax.ppermute(value, axis, [(i, (i + by) % length) for i in range(length)])


def exchange(array, axis):
    parts = lax.axis_size("head")
    here = lax.axis_index("head")
    size = array.shape[axis] // parts
    pieces = [
        lax.dynamic_slice_in_dim(array, (here + k) % parts * size, size, axis)
        for k in range(parts)
    ]
    return pieces[:1] + [shift(piece, "head", k) for k, piece in enumerate(pieces) if k]


def relays(length):
    back, onto, inside = [], [], []
    for c in range(CORES - 1, length, CORES):
        row, chip = divmod(c // CORES, LINE)
        relay = (row * LINE + (chip - 1) % LINE) * CORES + CORES - 1
        back.append((c, relay))
        onto.append((relay, (c + HOPS) % length))
        inside.append((c - 1, c))
    return back, onto, inside


def ring(value):
    back, onto, inside = relays(lax.axis_size("ctx"))
    one = shift(value, "ctx", 1)
    passed = lax.ppermute(value, "ctx", back)
    two = shift(one, "ctx", 1)
    far = lax.ppermute(passed, "ctx", onto)
    close = lax.ppermute(two, "ctx", inside)
    far_side = (lax.axis_index("ctx") % CORES == 0).astype(jnp.int32).reshape(1)
    return one, two, pick(far_side, far, close)


def body(queries, keys, values, directions):
    parts = lax.axis_size("head")
    here = lax.axis_index("head").astype(jnp.int32).reshape(1)
    position = lax.axis_index("ctx")
    oks = [(position >= d).astype(jnp.int32).reshape(1) for d in range(1, HOPS + 1)]
    w = exchange(directions, 1)
    v = exchange(values, 1)
    k = exchange(keys, 1)
    q = exchange(queries, 1)
    v = assemble(here, v)
    low_a, ft_a, w, chain = first_frames(here, w)
    low_b, ft_b, pt = second_frames(w, chain)
    frames = (low_a, ft_a, low_b, ft_b)
    kp = turn(here, k, w, frames, pt, True)
    z = turn(here, q, w, frames, pt, False)
    acc, stat = attend_local(z, kp, v)
    vs = ring(v)
    ks = ring(kp)
    acc, stat, z = attend_hop(oks[0], z, ks[0], vs[0], acc, stat)
    state = (jnp.concatenate(oks[1:]), here, z, (ks[1], vs[1]), (ks[2], vs[2]), acc, stat)
    pieces = attend_last(*state, tuple(range(1, parts)), parts)
    pieces = [shift(piece, "head", k + 1) for k, piece in enumerate(pieces)]
    pieces = list(attend_last(*state, (0,), parts)) + pieces
    rows, width = pieces[0].shape
    result = jnp.zeros((rows, width * parts), bf16)
    for k, piece in enumerate(pieces):
        result = lax.dynamic_update_slice(result, piece, (0, (here[0] + parts - k) % parts * width))
    return result


def solution(mesh):
    spec = P(("ctx", "head"), None)
    return jax.shard_map(
        body, mesh=mesh, in_specs=(spec,) * 4, out_specs=spec, check_vma=False
    )
```

```python
import math
import jax
import jax.numpy as jnp
from jax import lax
from jax.experimental import pallas as pl
from jax.experimental.pallas import tpu as pltpu
from jax.sharding import PartitionSpec as P

DH = 128
SUB = 128
bf16 = jnp.bfloat16
f32 = jnp.float32
VMEM = pl.BlockSpec(memory_space=pltpu.VMEM)
SMEM = pl.BlockSpec(memory_space=pltpu.SMEM)
GRANT = 24 << 20
COST = 1000


near = pltpu.VMEM


def keep_near(x):
    return pltpu.with_memory_space_constraint(x, pltpu.VMEM)


def keep_far(x):
    return pltpu.with_memory_space_constraint(x, pltpu.HBM)


def dot(a, b):
    return jnp.dot(a, b, preferred_element_type=f32)


def dot_t(a, b):
    return lax.dot_general(a, b, (((1,), (1,)), ((), ())), preferred_element_type=f32)


def halves(x):
    high = x.astype(bf16)
    return high, (x - high.astype(f32)).astype(bf16)


def thirds(x):
    high = x.astype(bf16)
    rest = x - high.astype(f32)
    middle = rest.astype(bf16)
    return high, middle, (rest - middle.astype(f32)).astype(bf16)


def dot6(a, b):
    return dot(
        jnp.concatenate([a[0], a[1], a[2], a[0], a[1], a[0]], axis=1),
        jnp.concatenate([b[0], b[0], b[0], b[1], b[1], b[2]], axis=0),
    )


def dot3(a, b):
    return dot(
        jnp.concatenate([a[0], a[1], a[0]], axis=1), jnp.concatenate([b[0], b[0], b[1]], axis=0)
    )


def put_chunks(here_ref, chunks, out_ref, part=None):
    here = here_ref[0]
    parts = len(chunks)
    rows = chunks[0].shape[-2]
    for k, chunk in enumerate(chunks):
        start = pl.multiple_of((here + parts - k) % parts * rows, rows)
        out_ref[pl.ds(start, rows), :] = chunk[...] if part is None else chunk[part]


def assemble(here, chunks):
    rows, width = chunks[0].shape
    return pl.pallas_call(
        lambda here_ref, *refs: put_chunks(here_ref, refs[:-1], refs[-1]),
        out_shape=near((rows * len(chunks), width), bf16),
        in_specs=[SMEM] + [VMEM] * len(chunks),
        out_specs=VMEM,
        cost_estimate=pl.CostEstimate(flops=COST, bytes_accessed=COST, transcendentals=COST),
        compiler_params=pltpu.CompilerParams(vmem_limit_bytes=GRANT),
        name="assemble",
    )(here, *map(keep_near, chunks))


def pick_kernel(first_ref, one_ref, two_ref, out_ref):
    @pl.when(first_ref[0] > 0)
    def _():
        out_ref[...] = one_ref[...]

    @pl.when(first_ref[0] == 0)
    def _():
        out_ref[...] = two_ref[...]


def pick(first, one, two):
    return pl.pallas_call(
        pick_kernel,
        out_shape=near(one.shape, one.dtype),
        in_specs=[SMEM] + [VMEM] * 2,
        out_specs=VMEM,
        cost_estimate=pl.CostEstimate(flops=COST, bytes_accessed=COST, transcendentals=COST),
        compiler_params=pltpu.CompilerParams(vmem_limit_bytes=GRANT),
        name="pick",
    )(first, keep_near(one), keep_near(two))


def frames_kernel(*refs, group, first):
    if first:
        here_ref, chunks = refs[0], refs[1:-4]
        v_ref, ft_ref, w_ref, chain_ref = refs[-4:]
        put_chunks(here_ref, chunks, w_ref)
        base = 0
    else:
        w_ref, old_ref, v_ref, ft_ref, pt_ref, chain_ref = refs
        base = w_ref.shape[0] - v_ref.shape[0]
    heads = w_ref.shape[1] // DH
    steps = v_ref.shape[0] // (SUB * group)
    rows = lax.broadcasted_iota(jnp.int32, (SUB, SUB), 0)
    cols = lax.broadcasted_iota(jnp.int32, (SUB, SUB), 1)
    diagonal = rows == cols
    unit = jnp.where(diagonal, 1.0, 0.0).astype(f32)
    for h in range(heads):
        chain_ref[h] = unit if first else old_ref[h]

    def one(step, carry):
        pairs = [(g, h) for g in range(group) for h in range(heads)]

        def at(g, h):
            start = pl.multiple_of((step * group + g) * SUB, SUB)
            return (pl.ds(start, SUB), pl.ds(h * DH, DH))

        def source(g, h):
            start = pl.multiple_of((step * group + g) * SUB + base, SUB)
            return (pl.ds(start, SUB), pl.ds(h * DH, DH))

        w = [w_ref[source(*p)] for p in pairs]
        wt = [x.T for x in w]
        gram = [dot(x, t) for x, t in zip(w, wt)]
        lower, inverse, matrix = [], [], []
        for x in gram:
            onto = jnp.where(diagonal, x, 0.0)
            down = 2.0 / (jnp.sum(onto, axis=1, keepdims=True) + 1e-6)
            across = 2.0 / (jnp.sum(onto, axis=0, keepdims=True) + 1e-6)
            near = jnp.where((rows == cols + 1) & (rows % 2 == 1), x, 0.0)
            inverse.append(jnp.where(diagonal, down, 0.0) - near * down * across)
            lower.append(halves(x))
            matrix.append(jnp.where(rows > cols, x, jnp.where(diagonal, 0.5 * (x + 1e-6), 0.0)))
        size = 2
        while size < SUB:
            band = (rows // (2 * size) == cols // (2 * size)) & (rows // size > cols // size)
            split = [halves(x) for x in inverse]
            part = [
                (jnp.where(band, x[0], 0).astype(bf16), jnp.where(band, x[1], 0).astype(bf16))
                for x in lower
            ]
            half = [halves(dot3(x, y)) for x, y in zip(split, part)]
            inverse = [x - dot3(y, z) for x, y, z in zip(inverse, half, split)]
            size *= 2
        split = [halves(x) for x in inverse]
        guess = [
            dot(jnp.concatenate(x, axis=1), jnp.concatenate([y, y], axis=0))
            for x, y in zip(split, w)
        ]
        short = [
            (y.astype(f32) - dot6(thirds(m), thirds(x))).astype(bf16)
            for m, x, y in zip(matrix, guess, w)
        ]
        solved = [x + dot(y[0], z) for x, y, z in zip(guess, split, short)]
        whole = [
            thirds(
                unit
                - dot(jnp.concatenate([t, t, t], axis=1), jnp.concatenate(thirds(v), axis=0))
            )
            for t, v in zip(wt, solved)
        ]
        for i, p in enumerate(pairs):
            v_ref[at(*p)] = solved[i]
        frames = [thirds(chain_ref[h]) for h in range(heads)]
        for i, p in enumerate(pairs):
            h = p[1]
            ft_ref[at(*p)] = frames[h][0]
            moved = dot6(whole[i], frames[h])
            if p[0] == group - 1:
                chain_ref[h] = moved
            frames[h] = thirds(moved)
        return carry

    lax.fori_loop(0, steps, one, 0)
    if not first:
        for h in range(heads):
            pt_ref[:, h * DH : (h + 1) * DH] = chain_ref[h].astype(bf16)


def first_frames(here, chunks, group=3):
    rows, width = chunks[0].shape
    rows *= len(chunks)
    half = rows // 2
    return pl.pallas_call(
        lambda *refs: frames_kernel(*refs, group=group, first=True),
        out_shape=(
            near((half, width), f32),
            near((half, width), bf16),
            near((rows, width), bf16),
            near((width // DH, DH, DH), f32),
        ),
        in_specs=[SMEM] + [VMEM] * len(chunks),
        out_specs=(VMEM,) * 4,
        cost_estimate=pl.CostEstimate(flops=COST, bytes_accessed=COST, transcendentals=COST),
        compiler_params=pltpu.CompilerParams(vmem_limit_bytes=GRANT),
        name="first_frames",
    )(here, *map(keep_near, chunks))


def second_frames(w, chain, group=3):
    rows, width = w.shape
    half = rows // 2
    return pl.pallas_call(
        lambda *refs: frames_kernel(*refs, group=group, first=False),
        out_shape=(
            near((half, width), f32),
            near((half, width), bf16),
            near((DH, width), bf16),
        ),
        in_specs=[VMEM] * 2,
        out_specs=(VMEM,) * 3,
        scratch_shapes=[pltpu.VMEM((width // DH, DH, DH), f32)],
        cost_estimate=pl.CostEstimate(flops=COST, bytes_accessed=COST, transcendentals=COST),
        compiler_params=pltpu.CompilerParams(vmem_limit_bytes=GRANT),
        name="second_frames",
    )(keep_near(w), keep_near(chain))


def turn_kernel(here_ref, *refs, group, tail):
    chunks, (w_ref, v0_ref, ft0_ref, v1_ref, ft1_ref, pt_ref, o_ref, x_ref) = refs[:-8], refs[-8:]
    put_chunks(here_ref, chunks, x_ref, 0 if tail else 1)
    length, width = x_ref.shape
    heads = width // DH
    half = length // 2
    rows = lax.broadcasted_iota(jnp.int32, (SUB, SUB), 0)
    cols = lax.broadcasted_iota(jnp.int32, (SUB, SUB), 1)
    seen = rows >= cols

    def one(step, base, v_ref, ft_ref):
        places, inner = [], []
        for g in range(group):
            start = pl.multiple_of((step * group + g) * SUB, SUB)
            for h in range(heads):
                inner.append((pl.ds(start, SUB), pl.ds(h * DH, DH)))
                places.append((pl.ds(start + base, SUB), pl.ds(h * DH, DH)))
        x = [x_ref[p] for p in places]
        onto = [thirds(jnp.where(seen, dot_t(y, w_ref[p]), 0.0)) for y, p in zip(x, places)]
        turned = [
            (y.astype(f32) - dot6(z, thirds(v_ref[p]))).astype(bf16)
            for y, z, p in zip(x, onto, inner)
        ]
        for y, p, i in zip(turned, places, inner):
            o_ref[p] = dot(y, ft_ref[i]).astype(bf16)

    for base, v_ref, ft_ref in ((0, v0_ref, ft0_ref), (half, v1_ref, ft1_ref)):

        def loop(step, carry):
            one(step, base, v_ref, ft_ref)
            return carry

        lax.fori_loop(0, half // (SUB * group), loop, 0)
    if tail:
        o_ref[length:, :] = pt_ref[...]


def turn(here, chunks, w, parts, pt, tail, group=3):
    rows, width = w.shape
    return pl.pallas_call(
        lambda *refs: turn_kernel(*refs, group=group, tail=tail),
        out_shape=near((rows + (DH if tail else 0), width), bf16),
        in_specs=[SMEM] + [VMEM] * (6 + len(chunks)),
        out_specs=VMEM,
        scratch_shapes=[pltpu.VMEM((rows, width), bf16)],
        cost_estimate=pl.CostEstimate(flops=COST, bytes_accessed=COST, transcendentals=COST),
        compiler_params=pltpu.CompilerParams(vmem_limit_bytes=GRANT),
        name="turn_keys" if tail else "turn_queries",
    )(here, *map(keep_near, (*chunks, w, *parts, pt)))


SCALE = math.log2(math.e) / math.sqrt(DH)
TILE = 256
SPAN = 256

BLANK = -1e30


def lanes_of(h):
    return slice(h * DH, (h + 1) * DH)


def pack_stats(columns):
    lane = lax.broadcasted_iota(jnp.int32, (columns[0].shape[0], DH), 1)
    out = jnp.zeros(lane.shape, f32)
    for i, c in enumerate(columns):
        out = jnp.where(lane == i, c, out)
    return out


def score(z, k, s_ref, m_ref, start=None):
    s = dot_t(z, k)
    rows, size = s.shape
    if start is not None:
        low = s[:, : size - rows]
        edge = s[:, size - rows :]
        seen = lax.broadcasted_iota(jnp.int32, edge.shape, 0) >= lax.broadcasted_iota(
            jnp.int32, edge.shape, 1
        )
        edge = jnp.where(seen, edge, BLANK)
        s = jnp.concatenate([low, edge], axis=1) if size > rows else edge
    s_ref[:, :size] = s
    m_ref[...] = jnp.broadcast_to(jnp.max(s, axis=1, keepdims=True), m_ref.shape)


def weigh(v, s_ref, m_ref):
    size = v.shape[0]
    best = m_ref[:, :1]
    p = jnp.exp2((s_ref[:, :size] - best) * SCALE).astype(bf16)
    return best, dot(p, jnp.concatenate([v, jnp.ones_like(v)], axis=1))


def scratch(heads, length, tile):
    return [pltpu.VMEM((tile, length), f32) for _ in range(heads)] + [
        pltpu.VMEM((tile, DH), f32) for _ in range(heads)
    ]


def local_kernel(q_ref, k_ref, v_ref, acc_ref, stat_ref, *work):
    length, width = q_ref.shape
    heads = width // DH
    tiles = length // TILE

    def first(i, h):
        size = (i + 1) * TILE
        score(
            q_ref[i * TILE : size, lanes_of(h)],
            k_ref[:size, lanes_of(h)],
            work[h],
            work[heads + h],
            i * TILE,
        )

    order = [(i, h) for i in range(tiles) for h in range(heads)]
    first(*order[0])
    columns = []
    for n, (i, h) in enumerate(order):
        if n + 1 < len(order):
            first(*order[n + 1])
        size = (i + 1) * TILE
        best, both = weigh(v_ref[:size, lanes_of(h)], work[h], work[heads + h])
        acc_ref[i * TILE : size, lanes_of(h)] = both[:, :DH]
        columns += [best, both[:, DH : DH + 1]]
        if h == heads - 1:
            stat_ref[i * TILE : size, :] = pack_stats(columns)
            columns = []


def attend_local(zq, kp, v):
    rows, width = zq.shape
    return pl.pallas_call(
        local_kernel,
        out_shape=(
            pltpu.HBM((rows, width), f32),
            pltpu.HBM((rows, DH), f32),
        ),
        in_specs=[VMEM] * 3,
        out_specs=(VMEM,) * 2,
        scratch_shapes=scratch(width // DH, rows, TILE),
        cost_estimate=pl.CostEstimate(flops=COST, bytes_accessed=COST, transcendentals=COST),
        compiler_params=pltpu.CompilerParams(vmem_limit_bytes=GRANT),
        name="attend_local",
    )(keep_near(zq), keep_near(kp), keep_near(v))


def merge(ok, best, both, stat, acc, h, wide):
    old = stat[:, 2 * h : 2 * h + 1]
    top = jnp.where(ok, jnp.maximum(old, best), old)
    keep = jnp.exp2((old - top) * SCALE)
    gain = jnp.where(ok, jnp.exp2((best - top) * SCALE), 0.0)
    sums = both[:, DH:] if wide else both[:, DH : DH + 1]
    total = stat[:, 2 * h + 1 : 2 * h + 2] * keep + sums * gain
    return top, acc * keep + both[:, :DH] * gain, total


def hop_kernel(ok_ref, here_ref, z_ref, k_ref, v_ref, acc_ref, stat_ref, *refs):
    out_ref, total_ref, turned_ref = refs[:3]
    own, work = refs[3:6], refs[6:]
    length, width = z_ref.shape
    heads = width // DH
    tiles = length // SPAN
    ok = ok_ref[0] > 0
    for h in range(heads):
        turned_ref[:, lanes_of(h)] = dot(z_ref[:, lanes_of(h)], k_ref[length:, lanes_of(h)]).astype(
            bf16
        )

    def rows_of(i):
        return pl.ds(pl.multiple_of(i * SPAN, SPAN), SPAN)

    def first(i, h):
        score(turned_ref[rows_of(i), lanes_of(h)], k_ref[:length, lanes_of(h)], work[h], work[heads + h])

    def one(i, more):
        columns = []
        for h in range(heads):
            if h + 1 < heads:
                first(i, h + 1)
            elif more:
                first(i + 1, 0)
            best, both = weigh(v_ref[:, lanes_of(h)], work[h], work[heads + h])
            top, acc, total = merge(
                ok, best, both, stat_ref[rows_of(i), :], acc_ref[rows_of(i), lanes_of(h)], h, False
            )
            out_ref[rows_of(i), lanes_of(h)] = acc
            columns += [top, total]
        total_ref[rows_of(i), :] = pack_stats(columns)

    first(0, 0)

    def step(i, carry):
        one(i, True)
        return carry

    lax.fori_loop(0, tiles - 1, step, 0)
    one(tiles - 1, False)
    piece = own[0].shape[0]
    place = pl.ds(pl.multiple_of(here_ref[0] * piece, piece), piece)
    for source, target in zip((out_ref, total_ref, turned_ref), own):
        target[...] = source[place, :]


def attend_hop(ok, here, z, kp, v, acc, stat, parts):
    rows, width = z.shape
    shapes = [
        pltpu.HBM((size, w), kind)
        for size in (rows, rows // parts)
        for w, kind in ((width, f32), (DH, f32), (width, bf16))
    ]
    return pl.pallas_call(
        hop_kernel,
        out_shape=shapes,
        in_specs=[SMEM] * 2 + [VMEM] * 5,
        out_specs=(VMEM,) * 6,
        scratch_shapes=scratch(width // DH, rows, SPAN),
        cost_estimate=pl.CostEstimate(flops=COST, bytes_accessed=COST, transcendentals=COST),
        compiler_params=pltpu.CompilerParams(vmem_limit_bytes=GRANT),
        name="attend_hop",
    )(ok, here, keep_near(z), keep_near(kp), v, keep_far(acc), keep_far(stat))


def last_kernel(ok_ref, here_ref, z_ref, *refs, targets, parts):
    pairs, refs = (refs[:2], refs[2:4]), refs[4:]
    acc_ref, stat_ref, out, work = refs[0], refs[1], refs[2 : 2 + len(targets)], refs[2 + len(targets) :]
    done_ref, turned_ref, work = work[0], work[1], work[2:]
    length, width = pairs[0][1].shape
    heads = width // DH
    piece = length // parts
    order = [(d, h) for d in range(len(pairs)) for h in range(heads)]

    def rows_of(i):
        if z_ref.shape[0] == piece:
            return slice(None)
        return pl.ds(pl.multiple_of((here_ref[0] + targets[0] + i) % parts * piece, piece), piece)

    def first(i, d, h):
        k_ref = pairs[d][0]
        old = turned_ref[:, lanes_of(h)] if d else z_ref[rows_of(i), lanes_of(h)]
        z = dot(old, k_ref[length:, lanes_of(h)]).astype(bf16)
        turned_ref[:, lanes_of(h)] = z
        score(z, k_ref[:length, lanes_of(h)], work[h], work[heads + h])

    def one(i, carry):
        state = [None] * heads
        for n, (d, h) in enumerate(order):
            if n + 1 < len(order):
                first(i, *order[n + 1])
            elif len(targets) > 1:
                first(jnp.minimum(i + 1, len(targets) - 1), *order[0])
            best, both = weigh(pairs[d][1][:, lanes_of(h)], work[h], work[heads + h])
            if d == 0:
                stat = stat_ref[rows_of(i), :]
                old = stat[:, 2 * h : 2 * h + 1]
                total = stat[:, 2 * h + 1 : 2 * h + 2]
                acc = acc_ref[rows_of(i), lanes_of(h)]
            else:
                old, acc, total = state[h]
            ok = ok_ref[d] > 0
            top = jnp.where(ok, jnp.maximum(old, best), old)
            keep = jnp.exp2((old - top) * SCALE)
            gain = jnp.where(ok, jnp.exp2((best - top) * SCALE), 0.0)
            acc = acc * keep + both[:, :DH] * gain
            total = total * keep + both[:, DH:] * gain
            state[h] = (top, acc, total)
            if d == len(pairs) - 1:
                done_ref[i, :, lanes_of(h)] = (acc / total).astype(bf16)
        return carry

    first(0, *order[0])
    lax.fori_loop(0, len(targets), one, 0)
    for i in range(len(targets)):
        out[i][...] = done_ref[i]


def attend_last(ok, here, z, near_pair, far_pair, acc, stat, targets, parts):
    rows, width = near_pair[1].shape
    piece = rows // parts
    return pl.pallas_call(
        lambda *refs: last_kernel(*refs, targets=targets, parts=parts),
        out_shape=tuple(
            (near if len(targets) == 1 else pltpu.HBM)((piece, width), bf16) for _ in targets
        ),
        in_specs=[SMEM] * 2 + [VMEM] * 7,
        out_specs=(VMEM,) * len(targets),
        scratch_shapes=[
            pltpu.VMEM((len(targets), piece, width), bf16),
            pltpu.VMEM((piece, width), bf16),
        ]
        + scratch(width // DH, rows, piece),
        cost_estimate=pl.CostEstimate(flops=COST, bytes_accessed=COST, transcendentals=COST),
        compiler_params=pltpu.CompilerParams(vmem_limit_bytes=GRANT),
    )(ok, here, keep_far(z), keep_far(near_pair[0]), *map(keep_near, (near_pair[1], *far_pair)), keep_far(acc), keep_far(stat))


HOPS = 3
CORES = 2
LINE = 4


def shift(value, axis, by):
    length = lax.axis_size(axis)
    return lax.ppermute(value, axis, [(i, (i + by) % length) for i in range(length)])


def exchange(*arrays):
    parts = lax.axis_size("head")
    here = lax.axis_index("head")
    size = arrays[0].shape[1] // parts

    def cut(k):
        found = [
            lax.dynamic_slice_in_dim(array, (here + k) % parts * size, size, 1) for array in arrays
        ]
        return found[0] if len(found) == 1 else jnp.stack(found)

    pieces = [cut(k) for k in range(parts)]
    return pieces[:1] + [shift(piece, "head", k) for k, piece in enumerate(pieces) if k]


def relays(length):
    back, onto, inside = [], [], []
    for c in range(CORES - 1, length, CORES):
        row, chip = divmod(c // CORES, LINE)
        relay = (row * LINE + (chip - 1) % LINE) * CORES + CORES - 1
        back.append((c, relay))
        onto.append((relay, (c + HOPS) % length))
        inside.append((c - 1, c))
    return back, onto, inside


def ring(value):
    found = []
    for _ in range(HOPS):
        value = shift(value, "ctx", 1)
        found.append(value)
    return found


def relayed(value):
    back, onto, inside = relays(lax.axis_size("ctx"))
    one = shift(value, "ctx", 1)
    passed = lax.ppermute(value, "ctx", back)
    two = shift(one, "ctx", 1)
    far = lax.ppermute(passed, "ctx", onto)
    close = lax.ppermute(two, "ctx", inside)
    far_side = (lax.axis_index("ctx") % CORES == 0).astype(jnp.int32).reshape(1)
    return one, two, pick(far_side, far, close)


def body(queries, keys, values, directions):
    parts = lax.axis_size("head")
    here = lax.axis_index("head").astype(jnp.int32).reshape(1)
    position = lax.axis_index("ctx")
    oks = [(position >= d).astype(jnp.int32).reshape(1) for d in range(1, HOPS + 1)]
    w = exchange(directions)
    v = exchange(values)
    both = exchange(keys, queries)
    v = assemble(here, v)
    low_a, ft_a, w, chain = first_frames(here, w)
    low_b, ft_b, pt = second_frames(w, chain)
    frames = (low_a, ft_a, low_b, ft_b)
    kp = turn(here, both, w, frames, pt, True)
    z = turn(here, both, w, frames, pt, False)
    acc, stat = attend_local(z, kp, v)
    vs = ring(v)
    ks = relayed(kp)
    acc, stat, z, own_acc, own_stat, own_z = attend_hop(
        oks[0], here, z, ks[0], vs[0], acc, stat, parts
    )
    shared = ((ks[1], vs[1]), (ks[2], vs[2]))
    ok = jnp.concatenate(oks[1:])
    pieces = attend_last(ok, here, z, *shared, acc, stat, tuple(range(1, parts)), parts)
    pieces = [shift(piece, "head", k + 1) for k, piece in enumerate(pieces)]
    pieces = list(attend_last(ok, here, own_z, *shared, own_acc, own_stat, (0,), parts)) + pieces
    rows, width = pieces[0].shape
    result = jnp.zeros((rows, width * parts), bf16)
    for k, piece in enumerate(pieces):
        result = lax.dynamic_update_slice(result, piece, (0, (here[0] + parts - k) % parts * width))
    return result


def solution(mesh):
    spec = P(("ctx", "head"), None)
    return jax.shard_map(
        body, mesh=mesh, in_specs=(spec,) * 4, out_specs=spec, check_vma=False
    )
```
